32 devices in a mesh: segment: 2 (over x), dp: 16 (over z, y, core).
Axes of the slice: x: 2, y: 2, z: 4, core: 2. Of those that a mesh axis runs over, the one named last changes fastest.
Arguments:
- fine_inflow: bfloat16 [2, 16, 16, 16, 256], P('segment', 'dp'), may hold values from -250 to 250
- coarse_inflow: bfloat16 [2, 16, 8, 8, 512], P('segment', 'dp'), may hold values from -250 to 250
- fine_entries: bfloat16 [3, 16, 16, 16, 256], P(None, 'dp'), may hold values from -250 to 250
- fine_pending: bfloat16 [2, 2, 16, 16, 16, 256], P('segment', None, 'dp'), may hold values from -250 to 250, as said below
- coarse_pending: bfloat16 [2, 1, 16, 8, 8, 512], P('segment', None, 'dp'), may hold values from -250 to 250, as said below
- fine_kernels: bfloat16 [2, 2, 3, 3, 256, 256], P('segment'), may hold values from -0.125 to 0.125
- fine_mixing: bfloat16 [2, 256, 256], P('segment'), may hold values from -0.375 to 0.375
- fine_gains: float32 [2, 2, 256], P('segment'), may hold values from 0.5 to 1.5
- fine_shifts: float32 [2, 2, 256], P('segment'), may hold values from -3 to 3
- coarse_kernel: bfloat16 [2, 3, 3, 512, 512], P('segment'), may hold values from -0.09375 to 0.09375
- coarse_mixing: bfloat16 [2, 512, 512], P('segment'), may hold values from -0.25 to 0.25
- coarse_gains: float32 [2, 512], P('segment'), may hold values from 0.5 to 1.5
- coarse_shifts: float32 [2, 512], P('segment'), may hold values from -3 to 3
- descent_kernel: bfloat16 [2, 2, 256, 512], replicated, may hold values from -0.1875 to 0.1875
- upsample_kernel: bfloat16 [512, 2, 2, 256], replicated, may hold values from -0.25 to 0.25
Outputs:
- fine_stash: bfloat16 [2, 4, 16, 16, 16, 256], P('segment', None, 'dp')
- coarse_stash: bfloat16 [2, 4, 16, 8, 8, 512], P('segment', None, 'dp')
- fine_backlog: bfloat16 [2, 2, 16, 16, 16, 256], P('segment', None, 'dp')
- coarse_backlog: bfloat16 [2, 1, 16, 8, 8, 512], P('segment', None, 'dp')
The draws below stay inside these ranges and needn't reach their ends.
Inputs may be any that keep to these rules, and one draw needn't show every extreme that they name: `fine_pending`: at segments 1 and above only the first 1 slots are read. `coarse_pending`: at segments below 1 only the first 0 slots are read.
All inputs are finite; a program needn't handle non-finite values.
Results may differ from the reference program's by a relative error of at most 0.017.
Values may be sent and summed in bfloat16 or wider, within the bound.
A program may use at most 64 MiB of HBM per device.

```python
import jax
import jax.numpy as jnp
from jax import lax

FINE_CH = 256
COARSE_CH = 512
TILE = 16
TICKS = 4
CTILE = 8
HOLD_FINE = 2
RECV_FINE = 1
HOLD_COARSE = 1
RECV_COARSE = 0
N_SEGMENT = 2
N_DP = 16


def spread_tiles(key, tile_shape, dp_dim):
    base_key, rows_key, cols_key = jax.random.split(key, 3)
    normal_part = jnp.clip(jax.random.normal(base_key, tile_shape, jnp.float32), -6.0, 6.0)
    dp_place = lax.broadcasted_iota(jnp.float32, tile_shape, dp_dim)
    rising = 0.4 * jnp.exp(jnp.log(6.0) * dp_place / (N_DP - 1))
    row_scale = jnp.exp(jax.random.uniform(rows_key, tile_shape[:-1] + (1,), jnp.float32, jnp.log(0.3), jnp.log(3.0)))
    columns = jnp.exp(jax.random.uniform(cols_key, (tile_shape[-1],), jnp.float32, jnp.log(0.5), jnp.log(5.0)))
    return (normal_part * rising * row_scale * columns).astype(jnp.bfloat16)


def draw_fine_inflow(key, part):
    return spread_tiles(jax.random.fold_in(key, 11), (N_SEGMENT, N_DP, TILE, TILE, FINE_CH), 1)


def draw_coarse_inflow(key, part):
    return spread_tiles(jax.random.fold_in(key, 12), (N_SEGMENT, N_DP, CTILE, CTILE, COARSE_CH), 1)


def draw_fine_entries(key, part):
    return spread_tiles(jax.random.fold_in(key, 13), (TICKS - 1, N_DP, TILE, TILE, FINE_CH), 1)


def draw_fine_pending(key, part):
    return spread_tiles(jax.random.fold_in(key, 14), (N_SEGMENT, HOLD_FINE, N_DP, TILE, TILE, FINE_CH), 2)


def draw_coarse_pending(key, part):
    return spread_tiles(jax.random.fold_in(key, 15), (N_SEGMENT, HOLD_COARSE, N_DP, CTILE, CTILE, COARSE_CH), 2)


def block_scale(stream_key, shape, cuts, low, top_value):
    level, own = 1.0, jax.random.fold_in(stream_key, 6)
    for dim, parts in cuts:
        draws = jnp.exp(jax.random.uniform(jax.random.fold_in(own, dim), (parts,), jnp.float32, low / len(cuts), top_value / len(cuts)))
        level = level * jnp.repeat(draws, shape[dim] // parts).reshape([-1 if axis == dim else 1 for axis in range(len(shape))])
    return level


def bell_draw(key, extent, width, bound, pieces=(), kind=jnp.bfloat16):
    loudness = block_scale(key, extent, pieces, -0.22, 0.18) if pieces else 1.0
    array = jax.random.normal(key, extent, jnp.float32) * width * loudness
    return jnp.minimum(jnp.maximum(array, -bound), bound).astype(kind)


def setup_inputs(seed: int = 0) -> dict:
    seeds = jax.random.split(jax.random.key(seed), 16)
    return {
        "fine_inflow": draw_fine_inflow(jax.random.fold_in(seeds[15], 71), 0),
        "coarse_inflow": draw_coarse_inflow(jax.random.fold_in(seeds[15], 71), 0),
        "fine_entries": draw_fine_entries(jax.random.fold_in(seeds[15], 71), 0),
        "fine_pending": draw_fine_pending(jax.random.fold_in(seeds[15], 71), 0),
        "coarse_pending": draw_coarse_pending(jax.random.fold_in(seeds[15], 71), 0),
        "fine_kernels": bell_draw(seeds[5], (N_SEGMENT, 2, 3, 3, FINE_CH, FINE_CH), (9 * FINE_CH) ** -0.5, 0.125, ((0, 2),)),
        "fine_mixing": bell_draw(seeds[6], (N_SEGMENT, FINE_CH, FINE_CH), FINE_CH ** -0.5, 0.375, ((0, 2),)),
        "fine_gains": jnp.clip(0.5 + 1.0 * jax.random.uniform(seeds[7], (N_SEGMENT, 2, FINE_CH), jnp.float32) ** block_scale(seeds[7], (N_SEGMENT, 2, FINE_CH), ((0, 2),), -0.2, 0.2), 0.5, 1.5),
        "fine_shifts": bell_draw(seeds[8], (N_SEGMENT, 2, FINE_CH), 0.5, 3.0, ((0, 2),), jnp.float32),
        "coarse_kernel": bell_draw(seeds[9], (N_SEGMENT, 3, 3, COARSE_CH, COARSE_CH), (9 * COARSE_CH) ** -0.5, 0.09375, ((0, 2),)),
        "coarse_mixing": bell_draw(seeds[10], (N_SEGMENT, COARSE_CH, COARSE_CH), COARSE_CH ** -0.5, 0.25, ((0, 2),)),
        "coarse_gains": jnp.clip(0.5 + 1.0 * jax.random.uniform(seeds[11], (N_SEGMENT, COARSE_CH), jnp.float32) ** block_scale(seeds[11], (N_SEGMENT, COARSE_CH), ((0, 2),), -0.2, 0.2), 0.5, 1.5),
        "coarse_shifts": bell_draw(seeds[12], (N_SEGMENT, COARSE_CH), 0.5, 3.0, ((0, 2),), jnp.float32),
        "descent_kernel": bell_draw(seeds[13], (2, 2, FINE_CH, COARSE_CH), (4 * FINE_CH) ** -0.5, 0.1875),
        "upsample_kernel": bell_draw(seeds[14], (COARSE_CH, 2, 2, FINE_CH), COARSE_CH ** -0.5, 0.25),
    }


EPSILON = 1e-05

def convolve(images, kernel):
    return lax.conv_general_dilated(images, kernel, (1, 1), 'SAME', dimension_numbers=('NHWC', 'HWIO', 'NHWC'), preferred_element_type=jnp.float32)

def project(images, matrix):
    flat = images.reshape(-1, images.shape[-1])
    result = jnp.dot(flat, matrix, preferred_element_type=jnp.float32)
    return result.reshape(images.shape[:-1] + (matrix.shape[1],))

def descend(images, kernel):
    lowered = lax.conv_general_dilated(images, kernel, (2, 2), 'VALID', dimension_numbers=('NHWC', 'HWIO', 'NHWC'), preferred_element_type=jnp.float32)
    return lowered.astype(jnp.bfloat16)

def upsample(images, kernel):
    batches, height, breadth, coarse = images.shape
    fine_ch = kernel.shape[-1]
    spread = project(images, kernel.reshape(coarse, 4 * fine_ch))
    spread = spread.reshape(batches, height, breadth, 2, 2, fine_ch).transpose(0, 1, 3, 2, 4, 5)
    return spread.reshape(batches, 2 * height, 2 * breadth, fine_ch).astype(jnp.bfloat16)

def activate(values, gain, shift):
    center = lax.optimization_barrier(jnp.mean(values, axis=(0, 1, 2)))
    spread = lax.optimization_barrier(jnp.mean(jnp.square(values - center), axis=(0, 1, 2)))
    scaled = (values - center) * lax.rsqrt(spread + EPSILON) * gain + shift
    return jnp.maximum(scaled, 0.0).astype(jnp.bfloat16)

def reference(fine_inflow, coarse_inflow, fine_entries, fine_pending, coarse_pending, fine_kernels, fine_mixing, fine_gains, fine_shifts, coarse_kernel, coarse_mixing, coarse_gains, coarse_shifts, descent_kernel, upsample_kernel):
    half_depth = N_SEGMENT // 2
    fine_now = [fine_inflow[position] for position in range(N_SEGMENT)]
    coarse_now = [coarse_inflow[position] for position in range(N_SEGMENT)]
    sender_fine = [[fine_pending[pair_index, slot_index] for slot_index in range(HOLD_FINE)] for pair_index in range(half_depth)]
    receiver_fine = [[fine_pending[pair_index + half_depth, slot_index] for slot_index in range(RECV_FINE)] for pair_index in range(half_depth)]
    sender_coarse = [[coarse_pending[pair_index + half_depth, slot_index] for slot_index in range(HOLD_COARSE)] for pair_index in range(half_depth)]
    receiver_coarse = [[coarse_pending[pair_index, slot_index] for slot_index in range(RECV_COARSE)] for pair_index in range(half_depth)]
    fine_store = [[] for position in range(N_SEGMENT)]
    coarse_store = [[] for position in range(N_SEGMENT)]
    for tick_now in range(TICKS):
        if tick_now > 0:
            fine_last = [fine_store[position][-1] for position in range(N_SEGMENT)]
            coarse_last = [coarse_store[position][-1] for position in range(N_SEGMENT)]
            shifted_fine = [fine_entries[tick_now - 1]] + fine_last[:-1]
            shifted_coarse = [coarse_last[-1]] + coarse_last[:-1]
            shifted_fine[half_depth] = upsample(coarse_last[half_depth - 1], upsample_kernel)
            shifted_coarse[half_depth] = descend(fine_last[half_depth - 1], descent_kernel)
            fine_now = shifted_fine
            coarse_now = shifted_coarse
        for pair_index in range(half_depth):
            receiver_fine[pair_index].append(sender_fine[pair_index][tick_now])
            receiver_coarse[pair_index].append(sender_coarse[pair_index][tick_now])
        for position in range(N_SEGMENT):
            if position < half_depth:
                fine_input = fine_now[position]
                coarse_taken = receiver_coarse[position][tick_now]
                coarse_input = (project(coarse_now[position], coarse_mixing[position]) + coarse_taken.astype(jnp.float32)).astype(jnp.bfloat16)
            else:
                fine_taken = receiver_fine[position - half_depth][tick_now]
                fine_input = (project(fine_now[position], fine_mixing[position]) + fine_taken.astype(jnp.float32)).astype(jnp.bfloat16)
                coarse_input = coarse_now[position]
            fine_first = activate(convolve(fine_input, fine_kernels[position, 0]), fine_gains[position, 0], fine_shifts[position, 0])
            fine_out = activate(convolve(fine_first, fine_kernels[position, 1]), fine_gains[position, 1], fine_shifts[position, 1])
            coarse_out = activate(convolve(coarse_input, coarse_kernel[position]), coarse_gains[position], coarse_shifts[position])
            fine_store[position].append(fine_out)
            coarse_store[position].append(coarse_out)
            if position < half_depth:
                sender_fine[position].append(project(fine_out, fine_mixing[position]).astype(jnp.bfloat16))
            else:
                sender_coarse[position - half_depth].append(project(coarse_out, coarse_mixing[position]).astype(jnp.bfloat16))
    fine_stash = jnp.stack([jnp.stack(fine_store[position]) for position in range(N_SEGMENT)])
    coarse_stash = jnp.stack([jnp.stack(coarse_store[position]) for position in range(N_SEGMENT)])
    fine_zero = jnp.zeros_like(fine_inflow[0])
    coarse_zero = jnp.zeros_like(coarse_inflow[0])
    fine_rows = []
    coarse_rows = []
    for position in range(N_SEGMENT):
        if position < half_depth:
            fine_rows.append(jnp.stack(sender_fine[position][TICKS:TICKS + HOLD_FINE]))
            chosen = receiver_coarse[position][TICKS:TICKS + RECV_COARSE] + [coarse_zero] * (HOLD_COARSE - RECV_COARSE)
            coarse_rows.append(jnp.stack(chosen))
        else:
            chosen = receiver_fine[position - half_depth][TICKS:TICKS + RECV_FINE] + [fine_zero] * (HOLD_FINE - RECV_FINE)
            fine_rows.append(jnp.stack(chosen))
            coarse_rows.append(jnp.stack(sender_coarse[position - half_depth][TICKS:TICKS + HOLD_COARSE]))
    return (fine_stash, coarse_stash, jnp.stack(fine_rows), jnp.stack(coarse_rows))
```

```python
import functools

import jax
import jax.numpy as jnp
from jax import lax
from jax.experimental import pallas as pl
from jax.experimental.pallas import tpu as pltpu
from jax.sharding import PartitionSpec as P

EPSILON = 1e-05
LANES = 128
MESH = pl.DeviceIdType.MESH
F32 = jnp.float32
BF16 = jnp.bfloat16


def dot(a, b):
    return jnp.dot(a, b, preferred_element_type=F32)


def side_shifts(x, side):
    cells = x.shape[0]
    column = lax.rem(lax.broadcasted_iota(jnp.int32, x.shape, 0), side)
    before = jnp.where(column == 0, 0.0, pltpu.roll(x, 1, 0))
    after = jnp.where(column == side - 1, 0.0, pltpu.roll(x, cells - 1, 0))
    return before, x, after


def spread_taps(x, cols, side):
    cells, width = x.shape
    edge = jnp.zeros((side, width), F32)
    for dc, part in enumerate(side_shifts(x, side)):
        above = jnp.concatenate([edge, part[: cells - side]], axis=0)
        below = jnp.concatenate([part[side:], edge], axis=0)
        for dr, moved in enumerate((above, part, below)):
            start = (3 * dr + dc) * width
            cols[:, start : start + width] = moved.astype(BF16)


def put_stats(h, out):
    width = h.shape[1]
    rows = width // LANES
    total = jnp.sum(h, axis=0, keepdims=True)
    square = jnp.sum(h * h, axis=0, keepdims=True)
    for row in range(rows):
        lanes = slice(row * LANES, (row + 1) * LANES)
        out[row : row + 1, :] = total[:, lanes]
        out[rows + row : rows + row + 1, :] = square[:, lanes]


def norm_terms(total, gain, shift, count):
    rows = total.shape[0] // 2
    sums = jnp.concatenate([total[row : row + 1] for row in range(rows)], axis=1)
    squares = jnp.concatenate([total[rows + row : rows + row + 1] for row in range(rows)], axis=1)
    center = sums * (1.0 / count)
    spread = jnp.maximum(squares * (1.0 / count) - center * center, 0.0)
    scale = lax.rsqrt(spread + EPSILON) * gain
    return scale, shift - center * scale


def kernel(
    dims,
    fine_in, coarse_in, entries, fine_pend, coarse_pend,
    wf_hbm, mixf_hbm, fgain, fshift, wc_hbm, mixc_hbm, cgain, cshift, wd_hbm, wu_hbm,
    fst_out, cst_out, fback_out, cback_out,
    wf, mixf, wc, mixc, wd, wu,
    fin, cin, upin, skf, skc, fst, cst, dbuf,
    xs, hf, hc, upscr, colf, colc, zf, zc,
    statf, statc, gotf, gotc,
    load_sem, save_sem,
    fin_r, cin_r, up_r, skf_r, skc_r,
    fin_s, cin_s, up_s, skf_s, skc_s,
    gotf_r, gotc_r, statf_s, statc_s,
):
    nseg, ndp, ticks, fside, cside, hold_f, recv_f, hold_c, recv_c = dims
    half = nseg // 2
    seg = lax.axis_index("segment")
    me = lax.axis_index("dp")
    lower = seg < half
    upper = seg >= half
    turn = seg == half - 1
    after = lax.rem(seg + 1, nseg)
    mate = lax.rem(seg + half, nseg)

    def load(k, src, dst):
        return pltpu.make_async_copy(src, dst, load_sem.at[k])

    loads = [
        load(0, fine_in, fin.at[0]),
        load(1, wf_hbm, wf),
        load(2, mixf_hbm, mixf),
        load(3, coarse_in, cin.at[0]),
        load(4, mixc_hbm, mixc),
        load(5, wc_hbm, wc),
        load(6, wd_hbm, wd),
        load(7, wu_hbm, wu),
    ]
    for item in loads:
        item.start()
    own_entries = load(8, entries, fin.at[pl.ds(1, ticks - 1)])
    fine_lower = load(9, fine_pend, skf.at[pl.ds(0, hold_f)])
    coarse_upper = load(10, coarse_pend, skc.at[pl.ds(0, hold_c)])

    @pl.when(seg == 0)
    def _():
        own_entries.start()

    @pl.when(lower)
    def _():
        fine_lower.start()
        if recv_c:
            load(10, coarse_pend.at[pl.ds(0, recv_c)], skc.at[pl.ds(0, recv_c)]).start()

    @pl.when(upper)
    def _():
        coarse_upper.start()
        if recv_f:
            load(9, fine_pend.at[pl.ds(0, recv_f)], skf.at[pl.ds(0, recv_f)]).start()

    barrier = pltpu.get_barrier_semaphore()
    offsets = sorted({1 % nseg, nseg - 1, half})

    def greet(k, carry):
        pl.semaphore_signal(
            barrier, inc=1, device_id=(seg, lax.rem(me + k, ndp)), device_id_type=MESH
        )
        return carry

    lax.fori_loop(1, ndp, greet, 0)
    for offset in offsets:
        pl.semaphore_signal(
            barrier, inc=1, device_id=(lax.rem(seg + offset, nseg), me), device_id_type=MESH
        )
    zf[...] = jnp.zeros_like(zf)
    zc[...] = jnp.zeros_like(zc)
    pl.semaphore_wait(barrier, ndp - 1 + len(offsets))

    def push(src, dst, ssem, rsem, to):
        return pltpu.make_async_remote_copy(
            src_ref=src, dst_ref=dst, send_sem=ssem, recv_sem=rsem,
            device_id=(to, me), device_id_type=MESH,
        )

    def send_skf(j):
        return push(skf.at[j], skf.at[recv_f + j], skf_s.at[j], skf_r.at[j], mate)

    def send_skc(j):
        return push(skc.at[j], skc.at[recv_c + j], skc_s.at[j], skc_r.at[j], mate)

    def send_up(t):
        return push(cst.at[t], upin.at[t], up_s.at[t], up_r.at[t], after)

    def send_co(t):
        return push(cst.at[t], cin.at[t + 1], cin_s.at[t], cin_r.at[t], after)

    def send_down(t):
        return push(dbuf.at[t], cin.at[t + 1], cin_s.at[t], cin_r.at[t], after)

    def send_fo(t):
        return push(fst.at[t], fin.at[t + 1], fin_s.at[t], fin_r.at[t], after)

    def exchange(src, dst, ssem, rsem):
        def one(k, carry):
            pltpu.make_async_remote_copy(
                src_ref=src, dst_ref=dst.at[k - 1], send_sem=ssem, recv_sem=rsem,
                device_id=(seg, lax.rem(me + k, ndp)), device_id_type=MESH,
            ).start()
            return carry

        lax.fori_loop(1, ndp, one, 0)

    def whole(dst, ssem, rsem):
        return pltpu.make_async_remote_copy(
            src_ref=dst, dst_ref=dst, send_sem=ssem, recv_sem=rsem,
            device_id=(seg, lax.rem(me + 1, ndp)), device_id_type=MESH,
        )

    @pl.when(lower)
    def _():
        fine_lower.wait()
        for j in range(min(hold_f, ticks)):
            send_skf(j).start()
        if recv_c:
            load(10, coarse_pend.at[pl.ds(0, recv_c)], skc.at[pl.ds(0, recv_c)]).wait()

    @pl.when(upper)
    def _():
        coarse_upper.wait()
        for j in range(min(hold_c, ticks)):
            send_skc(j).start()
        if recv_f:
            load(9, fine_pend.at[pl.ds(0, recv_f)], skf.at[pl.ds(0, recv_f)]).wait()

    @pl.when(seg == 0)
    def _():
        own_entries.wait()

    for item in loads:
        item.wait()

    fcount = ndp * fside * fside
    ccount = ndp * cside * cside

    def save_f(t):
        return pltpu.make_async_copy(fst.at[t], fst_out.at[t], save_sem.at[0, t])

    def save_c(t):
        return pltpu.make_async_copy(cst.at[t], cst_out.at[t], save_sem.at[1, t])

    def tick(t, carry):
        @pl.when(lower)
        def _():
            @pl.when(jnp.logical_and(seg > 0, t > 0))
            def _():
                send_fo(t - 1).wait_recv()

            xs[...] = fin[t].astype(F32)

        @pl.when(upper)
        def _():
            @pl.when(jnp.logical_and(seg == half, t > 0))
            def _():
                send_up(t - 1).wait_recv()
                spread = dot(upin[t - 1], wu[...])
                width = spread.shape[1] // 4
                for a in range(2):
                    for c in range(2):
                        start = (2 * a + c) * width
                        part = spread[:, start : start + width].reshape(cside, cside, width)
                        for i in range(width // LANES):
                            lanes = slice(i * LANES, (i + 1) * LANES)
                            upscr[i, :, pl.ds(a * fside + c, cside, stride=2), :] = part[:, :, lanes]
                for i in range(width // LANES):
                    lanes = slice(i * LANES, (i + 1) * LANES)
                    fin[t, :, lanes] = upscr[i].reshape(fside * fside, LANES).astype(BF16)

            @pl.when(jnp.logical_and(seg != half, t > 0))
            def _():
                send_fo(t - 1).wait_recv()

            @pl.when(t >= recv_f)
            def _():
                send_skf(t - recv_f).wait_recv()

            xs[...] = (dot(fin[t], mixf[...]) + skf[t].astype(F32)).astype(BF16).astype(F32)

        spread_taps(xs[...], colf, fside)
        hf[...] = dot(colf[...], wf[0])
        put_stats(hf[...], statf.at[2 * t])
        exchange(statf.at[2 * t], gotf.at[2 * t], statf_s.at[2 * t], gotf_r.at[2 * t])

        @pl.when(t > 0)
        def _():
            send_co(t - 1).wait_recv()

        @pl.when(lower)
        def _():
            @pl.when(t >= recv_c)
            def _():
                send_skc(t - recv_c).wait_recv()

            hc[...] = (dot(cin[t], mixc[...]) + skc[t].astype(F32)).astype(BF16).astype(F32)

        @pl.when(upper)
        def _():
            hc[...] = cin[t].astype(F32)

        spread_taps(hc[...], colc, cside)
        hc[...] = dot(colc[...], wc[...])
        put_stats(hc[...], statc.at[t])
        exchange(statc.at[t], gotc.at[t], statc_s.at[t], gotc_r.at[t])

        whole(gotf.at[2 * t], statf_s.at[2 * t], gotf_r.at[2 * t]).wait_recv()
        total = statf[2 * t] + jnp.sum(gotf[2 * t], axis=0)
        scale, offset = norm_terms(total, fgain[0:1, :], fshift[0:1, :], fcount)
        xs[...] = jnp.maximum(hf[...] * scale + offset, 0.0).astype(BF16).astype(F32)
        spread_taps(xs[...], colf, fside)
        hf[...] = dot(colf[...], wf[1])
        put_stats(hf[...], statf.at[2 * t + 1])
        exchange(
            statf.at[2 * t + 1], gotf.at[2 * t + 1], statf_s.at[2 * t + 1], gotf_r.at[2 * t + 1]
        )

        whole(gotc.at[t], statc_s.at[t], gotc_r.at[t]).wait_recv()
        total = statc[t] + jnp.sum(gotc[t], axis=0)
        scale, offset = norm_terms(total, cgain[...], cshift[...], ccount)
        cst[t] = jnp.maximum(hc[...] * scale + offset, 0.0).astype(BF16)

        @pl.when(t < ticks - 1)
        def _():
            @pl.when(turn)
            def _():
                send_up(t).start()

            @pl.when(jnp.logical_not(turn))
            def _():
                send_co(t).start()

        save_c(t).start()

        @pl.when(upper)
        def _():
            skc[hold_c + t] = dot(cst[t], mixc[...]).astype(BF16)

            @pl.when(hold_c + t < ticks)
            def _():
                send_skc(hold_c + t).start()

        whole(gotf.at[2 * t + 1], statf_s.at[2 * t + 1], gotf_r.at[2 * t + 1]).wait_recv()
        total = statf[2 * t + 1] + jnp.sum(gotf[2 * t + 1], axis=0)
        scale, offset = norm_terms(total, fgain[1:2, :], fshift[1:2, :], fcount)
        fst[t] = jnp.maximum(hf[...] * scale + offset, 0.0).astype(BF16)

        @pl.when(t < ticks - 1)
        def _():
            @pl.when(turn)
            def _():
                width = fst.shape[2]
                for i in range(width // LANES):
                    lanes = slice(i * LANES, (i + 1) * LANES)
                    upscr[i] = fst[t, :, lanes].astype(F32).reshape(cside, 2 * fside, LANES)
                lowered = None
                for a in range(2):
                    for c in range(2):
                        for i in range(width // LANES):
                            part = upscr[i, :, pl.ds(a * fside + c, cside, stride=2), :]
                            part = part.reshape(cside * cside, LANES).astype(BF16)
                            start = (2 * a + c) * width + i * LANES
                            term = dot(part, wd[start : start + LANES, :])
                            lowered = term if lowered is None else lowered + term
                dbuf[t] = lowered.astype(BF16)
                send_down(t).start()

            @pl.when(jnp.logical_and(jnp.logical_not(turn), seg < nseg - 1))
            def _():
                send_fo(t).start()

        save_f(t).start()

        @pl.when(lower)
        def _():
            skf[hold_f + t] = dot(fst[t], mixf[...]).astype(BF16)

            @pl.when(hold_f + t < ticks)
            def _():
                send_skf(hold_f + t).start()

        return carry

    lax.fori_loop(0, ticks, tick, 0)

    def back_f(first, src):
        return pltpu.make_async_copy(src, fback_out.at[first], save_sem.at[2, first])

    def back_c(first, src):
        return pltpu.make_async_copy(src, cback_out.at[first], save_sem.at[3, first])

    lower_backs = [back_f(j, skf.at[ticks + j]) for j in range(hold_f)]
    lower_backs += [
        back_c(j, skc.at[ticks + j] if j < recv_c else zc) for j in range(hold_c)
    ]
    upper_backs = [
        back_f(j, skf.at[ticks + j] if j < recv_f else zf) for j in range(hold_f)
    ]
    upper_backs += [back_c(j, skc.at[ticks + j]) for j in range(hold_c)]

    @pl.when(lower)
    def _():
        for j in range(max(ticks - recv_c, 0), ticks):
            send_skc(j).wait_recv()
        for item in lower_backs:
            item.start()
        for j in range(ticks):
            send_skf(j).wait_send()
        for item in lower_backs:
            item.wait()

    @pl.when(upper)
    def _():
        for j in range(max(ticks - recv_f, 0), ticks):
            send_skf(j).wait_recv()
        for item in upper_backs:
            item.start()
        for j in range(ticks):
            send_skc(j).wait_send()
        for item in upper_backs:
            item.wait()

    @pl.when(turn)
    def _():
        for t in range(ticks - 1):
            send_up(t).wait_send()

    @pl.when(jnp.logical_and(jnp.logical_not(turn), seg < nseg - 1))
    def _():
        for t in range(ticks - 1):
            send_fo(t).wait_send()

    for t in range(ticks - 1):
        send_co(t).wait_send()
    for t in range(ticks):
        whole(gotf.at[2 * t], statf_s.at[2 * t], gotf_r.at[2 * t]).wait_send()
        whole(gotf.at[2 * t + 1], statf_s.at[2 * t + 1], gotf_r.at[2 * t + 1]).wait_send()
        whole(gotc.at[t], statc_s.at[t], gotc_r.at[t]).wait_send()
        save_f(t).wait()
        save_c(t).wait()


def on_device(
    fine_inflow, coarse_inflow, fine_entries, fine_pending, coarse_pending,
    fine_kernels, fine_mixing, fine_gains, fine_shifts,
    coarse_kernel, coarse_mixing, coarse_gains, coarse_shifts,
    descent_kernel, upsample_kernel,
):
    nseg = lax.axis_size("segment")
    ndp = lax.axis_size("dp")
    half = nseg // 2
    ticks = fine_entries.shape[0] + 1
    hold_f, hold_c = fine_pending.shape[1], coarse_pending.shape[1]
    recv_f, recv_c = 3 * half - hold_f, half - hold_c
    fside, fch = fine_inflow.shape[3], fine_inflow.shape[4]
    cside, cch = coarse_inflow.shape[3], coarse_inflow.shape[4]
    fcells, ccells = fside * fside, cside * cside
    dims = (nseg, ndp, ticks, fside, cside, hold_f, recv_f, hold_c, recv_c)
    frows, crows = 2 * fch // LANES, 2 * cch // LANES
    any_spec = pl.BlockSpec(memory_space=pl.ANY)
    vmem_spec = pl.BlockSpec(memory_space=pltpu.VMEM)
    dma = pltpu.SemaphoreType.DMA
    outs = pl.pallas_call(
        functools.partial(kernel, dims),
        out_shape=(
            jax.ShapeDtypeStruct((ticks, fcells, fch), BF16),
            jax.ShapeDtypeStruct((ticks, ccells, cch), BF16),
            jax.ShapeDtypeStruct((hold_f, fcells, fch), BF16),
            jax.ShapeDtypeStruct((hold_c, ccells, cch), BF16),
        ),
        in_specs=[any_spec] * 7 + [vmem_spec] * 2 + [any_spec] * 2 + [vmem_spec] * 2 + [any_spec] * 2,
        out_specs=(any_spec,) * 4,
        scratch_shapes=[
            pltpu.VMEM((2, 9 * fch, fch), BF16),
            pltpu.VMEM((fch, fch), BF16),
            pltpu.VMEM((9 * cch, cch), BF16),
            pltpu.VMEM((cch, cch), BF16),
            pltpu.VMEM((4 * fch, cch), BF16),
            pltpu.VMEM((cch, 4 * fch), BF16),
            pltpu.VMEM((ticks, fcells, fch), BF16),
            pltpu.VMEM((ticks, ccells, cch), BF16),
            pltpu.VMEM((ticks, ccells, cch), BF16),
            pltpu.VMEM((max(hold_f, recv_f) + ticks, fcells, fch), BF16),
            pltpu.VMEM((max(hold_c, recv_c) + ticks, ccells, cch), BF16),
            pltpu.VMEM((ticks, fcells, fch), BF16),
            pltpu.VMEM((ticks, ccells, cch), BF16),
            pltpu.VMEM((ticks, ccells, cch), BF16),
            pltpu.VMEM((fcells, fch), F32),
            pltpu.VMEM((fcells, fch), F32),
            pltpu.VMEM((ccells, cch), F32),
            pltpu.VMEM((fch // LANES, cside, 2 * fside, LANES), F32),
            pltpu.VMEM((fcells, 9 * fch), BF16),
            pltpu.VMEM((ccells, 9 * cch), BF16),
            pltpu.VMEM((fcells, fch), BF16),
            pltpu.VMEM((ccells, cch), BF16),
            pltpu.VMEM((2 * ticks, frows, LANES), F32),
            pltpu.VMEM((ticks, crows, LANES), F32),
            pltpu.VMEM((2 * ticks, ndp - 1, frows, LANES), F32),
            pltpu.VMEM((ticks, ndp - 1, crows, LANES), F32),
            dma((11,)),
            dma((4, max(ticks, hold_f, hold_c))),
            dma((ticks,)), dma((ticks,)), dma((ticks,)), dma((ticks,)), dma((ticks,)),
            dma((ticks,)), dma((ticks,)), dma((ticks,)), dma((ticks,)), dma((ticks,)),
            dma((2 * ticks,)), dma((ticks,)), dma((2 * ticks,)), dma((ticks,)),
        ],
        compiler_params=pltpu.CompilerParams(
            collective_id=0, has_side_effects=True, vmem_limit_bytes=56 << 20
        ),
    )(
        fine_inflow.reshape(fcells, fch),
        coarse_inflow.reshape(ccells, cch),
        fine_entries.reshape(ticks - 1, fcells, fch),
        fine_pending.reshape(hold_f, fcells, fch),
        coarse_pending.reshape(hold_c, ccells, cch),
        fine_kernels.reshape(2, 9 * fch, fch),
        fine_mixing.reshape(fch, fch),
        fine_gains.reshape(2, fch),
        fine_shifts.reshape(2, fch),
        coarse_kernel.reshape(9 * cch, cch),
        coarse_mixing.reshape(cch, cch),
        coarse_gains.reshape(1, cch),
        coarse_shifts.reshape(1, cch),
        descent_kernel.reshape(4 * fch, cch),
        upsample_kernel.reshape(cch, 4 * fch),
    )
    fst, cst, fback, cback = outs
    return (
        fst.reshape(1, ticks, 1, fside, fside, fch),
        cst.reshape(1, ticks, 1, cside, cside, cch),
        fback.reshape(1, hold_f, 1, fside, fside, fch),
        cback.reshape(1, hold_c, 1, cside, cside, cch),
    )


def solution(mesh):
    placed = (
        P("segment", "dp", None, None, None),
        P("segment", "dp", None, None, None),
        P(None, "dp", None, None, None),
        P("segment", None, "dp", None, None, None),
        P("segment", None, "dp", None, None, None),
        P("segment", None, None, None, None, None),
        P("segment", None, None),
        P("segment", None, None),
        P("segment", None, None),
        P("segment", None, None, None, None),
        P("segment", None, None),
        P("segment", None),
        P("segment", None),
        P(),
        P(),
    )
    return jax.shard_map(
        on_device,
        mesh=mesh,
        in_specs=placed,
        out_specs=(
            P("segment", None, "dp", None, None, None),
            P("segment", None, "dp", None, None, None),
            P("segment", None, "dp", None, None, None),
            P("segment", None, "dp", None, None, None),
        ),
        check_vma=False,
    )
```

```python
import functools

import jax
import jax.numpy as jnp
from jax import lax
from jax.experimental import pallas as pl
from jax.experimental.pallas import tpu as pltpu
from jax.sharding import PartitionSpec as P

EPSILON = 1e-05
LANES = 128
MESH = pl.DeviceIdType.MESH
F32 = jnp.float32
BF16 = jnp.bfloat16


def dot(a, b):
    return jnp.dot(a, b, preferred_element_type=F32)


def side_shifts(x, side):
    cells = x.shape[0]
    column = lax.rem(lax.broadcasted_iota(jnp.int32, x.shape, 0), side)
    before = jnp.where(column == 0, 0.0, pltpu.roll(x, 1, 0))
    after = jnp.where(column == side - 1, 0.0, pltpu.roll(x, cells - 1, 0))
    return before, x, after


def spread_taps(x, cols, side):
    cells, width = x.shape
    edge = jnp.zeros((side, width), F32)
    for dc, part in enumerate(side_shifts(x, side)):
        above = jnp.concatenate([edge, part[: cells - side]], axis=0)
        below = jnp.concatenate([part[side:], edge], axis=0)
        for dr, moved in enumerate((above, part, below)):
            start = (3 * dr + dc) * width
            cols[:, start : start + width] = moved.astype(BF16)


def put_stats(h, out):
    width = h.shape[1]
    rows = width // LANES
    total = jnp.sum(h, axis=0, keepdims=True)
    square = jnp.sum(h * h, axis=0, keepdims=True)
    for row in range(rows):
        lanes = slice(row * LANES, (row + 1) * LANES)
        out[row : row + 1, :] = total[:, lanes]
        out[rows + row : rows + row + 1, :] = square[:, lanes]


def norm_terms(total, gain, shift, count):
    rows = total.shape[0] // 2
    sums = jnp.concatenate([total[row : row + 1] for row in range(rows)], axis=1)
    squares = jnp.concatenate([total[rows + row : rows + row + 1] for row in range(rows)], axis=1)
    center = sums * (1.0 / count)
    spread = jnp.maximum(squares * (1.0 / count) - center * center, 0.0)
    scale = lax.rsqrt(spread + EPSILON) * gain
    return scale, shift - center * scale


def kernel(
    dims,
    fine_in, coarse_in, entries, fine_pend, coarse_pend,
    wf_hbm, mixf_hbm, fgain, fshift, wc_hbm, mixc_hbm, cgain, cshift, wd_hbm, wu_hbm,
    fst_out, cst_out, fback_out, cback_out,
    wf, mixf, wc, mixc, wd, wu,
    fin, cin, upin, skf, skc, fst, cst, dbuf,
    xs, hf, hc, upscr, colf, colc, zf, zc,
    statf, statc, gotf, gotc,
    wu4, wuf, load_sem, save_sem,
    fin_r, cin_r, up_r, skf_r, skc_r,
    fin_s, cin_s, up_s, skf_s, skc_s,
    gotf_r, gotc_r, statf_s, statc_s,
):
    nseg, ndp, ticks, fside, cside, hold_f, recv_f, hold_c, recv_c = dims
    half = nseg // 2
    seg = lax.axis_index("segment")
    me = lax.axis_index("dp")
    lower = seg < half
    upper = seg >= half
    turn = seg == half - 1
    after = lax.rem(seg + 1, nseg)
    mate = lax.rem(seg + half, nseg)

    def load(k, src, dst):
        return pltpu.make_async_copy(src, dst, load_sem.at[k])

    get_fine = load(0, fine_in, fin.at[0])
    get_wf0 = load(1, wf_hbm.at[0], wf.at[0])
    get_mixf = load(2, mixf_hbm, mixf)
    get_coarse = load(3, coarse_in, cin.at[0])
    get_mixc = load(4, mixc_hbm, mixc)
    get_wc = load(5, wc_hbm, wc)
    get_wf1 = load(6, wf_hbm.at[1], wf.at[1])
    get_wd = load(7, wd_hbm, wd)
    get_wu = load(11, wu_hbm, wu4)
    own_entries = load(8, entries, fin.at[pl.ds(1, ticks - 1)])
    own_fine = hold_f if hold_f > ticks else 0
    own_coarse = hold_c if hold_c > ticks else 0

    def own_pend(k, src, dst, count):
        return load(k, src.at[pl.ds(0, count)], dst.at[pl.ds(0, count)])

    barrier = pltpu.get_barrier_semaphore()
    offsets = sorted({1 % nseg, nseg - 1, half})

    def greet(k, carry):
        pl.semaphore_signal(
            barrier, inc=1, device_id=(seg, lax.rem(me + k, ndp)), device_id_type=MESH
        )
        return carry

    lax.fori_loop(1, ndp, greet, 0)
    for offset in offsets:
        pl.semaphore_signal(
            barrier, inc=1, device_id=(lax.rem(seg + offset, nseg), me), device_id_type=MESH
        )
    @pl.when(upper)
    def _():
        if recv_f:
            own_pend(9, fine_pend, skf, recv_f).start()

    for item in (get_fine, get_wf0, get_mixf, get_coarse, get_mixc, get_wc, get_wf1):
        item.start()

    @pl.when(lower)
    def _():
        if recv_c:
            own_pend(10, coarse_pend, skc, recv_c).start()
        if own_fine:
            own_pend(9, fine_pend, skf, own_fine).start()

    @pl.when(upper)
    def _():
        if own_coarse:
            own_pend(10, coarse_pend, skc, own_coarse).start()

    @pl.when(seg == 0)
    def _():
        own_entries.start()

    @pl.when(turn)
    def _():
        get_wd.start()

    @pl.when(seg == half)
    def _():
        get_wu.start()

    zf[...] = jnp.zeros_like(zf)
    zc[...] = jnp.zeros_like(zc)
    pl.semaphore_wait(barrier, ndp - 1 + len(offsets))

    def push(src, dst, ssem, rsem, to):
        return pltpu.make_async_remote_copy(
            src_ref=src, dst_ref=dst, send_sem=ssem, recv_sem=rsem,
            device_id=(to, me), device_id_type=MESH,
        )

    def send_skf(j):
        return push(skf.at[j], skf.at[recv_f + j], skf_s.at[j], skf_r.at[j], mate)

    def send_pend_f(j):
        return push(fine_pend.at[j], skf.at[recv_f + j], skf_s.at[j], skf_r.at[j], mate)

    def send_pend_c(j):
        return push(coarse_pend.at[j], skc.at[recv_c + j], skc_s.at[j], skc_r.at[j], mate)

    def send_skc(j):
        return push(skc.at[j], skc.at[recv_c + j], skc_s.at[j], skc_r.at[j], mate)

    def send_up(t):
        return push(cst.at[t], upin.at[t], up_s.at[t], up_r.at[t], after)

    def send_co(t):
        return push(cst.at[t], cin.at[t + 1], cin_s.at[t], cin_r.at[t], after)

    def send_down(t):
        return push(dbuf.at[t], cin.at[t + 1], cin_s.at[t], cin_r.at[t], after)

    def send_fo(t):
        return push(fst.at[t], fin.at[t + 1], fin_s.at[t], fin_r.at[t], after)

    def exchange(src, dst, ssem, rsem):
        def one(k, carry):
            pltpu.make_async_remote_copy(
                src_ref=src, dst_ref=dst.at[k - 1], send_sem=ssem, recv_sem=rsem,
                device_id=(seg, lax.rem(me + k, ndp)), device_id_type=MESH,
            ).start()
            return carry

        lax.fori_loop(1, ndp, one, 0)

    def whole(dst, ssem, rsem):
        return pltpu.make_async_remote_copy(
            src_ref=dst, dst_ref=dst, send_sem=ssem, recv_sem=rsem,
            device_id=(seg, lax.rem(me + 1, ndp)), device_id_type=MESH,
        )

    @pl.when(lower)
    def _():
        for j in range(min(hold_f, ticks)):
            send_pend_f(j).start()

    @pl.when(upper)
    def _():
        for j in range(min(hold_c, ticks)):
            send_pend_c(j).start()

    fcount = ndp * fside * fside
    ccount = ndp * cside * cside

    def save_f(t):
        return pltpu.make_async_copy(fst.at[t], fst_out.at[t], save_sem.at[0, t])

    def save_c(t):
        return pltpu.make_async_copy(cst.at[t], cst_out.at[t], save_sem.at[1, t])

    def first(t, *items):
        @pl.when(t == 0)
        def _():
            for item in items:
                item.wait()

    def tick(t, carry):
        first(t, get_fine, get_mixf)

        @pl.when(lower)
        def _():
            @pl.when(jnp.logical_and(seg > 0, t > 0))
            def _():
                send_fo(t - 1).wait_recv()

            xs[...] = fin[t].astype(F32)

        @pl.when(upper)
        def _():
            @pl.when(jnp.logical_and(seg == half, t > 0))
            def _():
                send_up(t - 1).wait_recv()
                spread = dot(upin[t - 1], wu[...])
                width = spread.shape[1] // 4
                for a in range(2):
                    for c in range(2):
                        start = (2 * a + c) * width
                        part = spread[:, start : start + width].reshape(cside, cside, width)
                        for i in range(width // LANES):
                            lanes = slice(i * LANES, (i + 1) * LANES)
                            upscr[i, :, pl.ds(a * fside + c, cside, stride=2), :] = part[:, :, lanes]
                for i in range(width // LANES):
                    lanes = slice(i * LANES, (i + 1) * LANES)
                    fin[t, :, lanes] = upscr[i].reshape(fside * fside, LANES).astype(BF16)

            @pl.when(jnp.logical_and(seg != half, t > 0))
            def _():
                send_fo(t - 1).wait_recv()

            if recv_f:
                first(t, own_pend(9, fine_pend, skf, recv_f))

            @pl.when(t >= recv_f)
            def _():
                send_skf(t - recv_f).wait_recv()

            xs[...] = (dot(fin[t], mixf[...]) + skf[t].astype(F32)).astype(BF16).astype(F32)

        spread_taps(xs[...], colf, fside)
        first(t, get_wf0)
        hf[...] = dot(colf[...], wf[0])
        put_stats(hf[...], statf.at[2 * t])
        exchange(statf.at[2 * t], gotf.at[2 * t], statf_s.at[2 * t], gotf_r.at[2 * t])

        first(t, get_coarse, get_mixc)

        @pl.when(t > 0)
        def _():
            send_co(t - 1).wait_recv()

        @pl.when(lower)
        def _():
            if recv_c:
                first(t, own_pend(10, coarse_pend, skc, recv_c))

            @pl.when(t >= recv_c)
            def _():
                send_skc(t - recv_c).wait_recv()

            hc[...] = (dot(cin[t], mixc[...]) + skc[t].astype(F32)).astype(BF16).astype(F32)

        @pl.when(upper)
        def _():
            hc[...] = cin[t].astype(F32)

        spread_taps(hc[...], colc, cside)
        first(t, get_wc)
        hc[...] = dot(colc[...], wc[...])
        put_stats(hc[...], statc.at[t])
        exchange(statc.at[t], gotc.at[t], statc_s.at[t], gotc_r.at[t])

        @pl.when(t == 0)
        def _():
            get_wf1.wait()

            @pl.when(turn)
            def _():
                get_wd.wait()

            @pl.when(seg == 0)
            def _():
                own_entries.wait()

            @pl.when(seg == half)
            def _():
                get_wu.wait()
                width = wu4.shape[3]
                depth = wuf.shape[1] // 4

                def rows_of(n, carry):
                    rows = pl.multiple_of(n * depth, depth)
                    piece = wu4[pl.ds(rows, depth)].astype(F32).reshape(4 * depth, width)
                    for i in range(width // LANES):
                        wuf[i] = piece[:, i * LANES : (i + 1) * LANES]
                    for q in range(4):
                        for i in range(width // LANES):
                            start = q * width + i * LANES
                            part = wuf[i, pl.ds(q, depth, stride=4), :]
                            wu[pl.ds(rows, depth), start : start + LANES] = part.astype(BF16)
                    return carry

                lax.fori_loop(0, wu4.shape[0] // depth, rows_of, 0)

        whole(gotf.at[2 * t], statf_s.at[2 * t], gotf_r.at[2 * t]).wait_recv()
        total = statf[2 * t] + jnp.sum(gotf[2 * t], axis=0)
        scale, offset = norm_terms(total, fgain[0:1, :], fshift[0:1, :], fcount)
        xs[...] = jnp.maximum(hf[...] * scale + offset, 0.0).astype(BF16).astype(F32)
        spread_taps(xs[...], colf, fside)
        hf[...] = dot(colf[...], wf[1])
        put_stats(hf[...], statf.at[2 * t + 1])
        exchange(
            statf.at[2 * t + 1], gotf.at[2 * t + 1], statf_s.at[2 * t + 1], gotf_r.at[2 * t + 1]
        )

        whole(gotc.at[t], statc_s.at[t], gotc_r.at[t]).wait_recv()
        total = statc[t] + jnp.sum(gotc[t], axis=0)
        scale, offset = norm_terms(total, cgain[...], cshift[...], ccount)
        cst[t] = jnp.maximum(hc[...] * scale + offset, 0.0).astype(BF16)

        @pl.when(t < ticks - 1)
        def _():
            @pl.when(turn)
            def _():
                send_up(t).start()

            @pl.when(jnp.logical_not(turn))
            def _():
                send_co(t).start()

        save_c(t).start()

        @pl.when(upper)
        def _():
            skc[hold_c + t] = dot(cst[t], mixc[...]).astype(BF16)

            @pl.when(hold_c + t < ticks)
            def _():
                send_skc(hold_c + t).start()

        whole(gotf.at[2 * t + 1], statf_s.at[2 * t + 1], gotf_r.at[2 * t + 1]).wait_recv()
        total = statf[2 * t + 1] + jnp.sum(gotf[2 * t + 1], axis=0)
        scale, offset = norm_terms(total, fgain[1:2, :], fshift[1:2, :], fcount)
        fst[t] = jnp.maximum(hf[...] * scale + offset, 0.0).astype(BF16)

        @pl.when(t < ticks - 1)
        def _():
            @pl.when(turn)
            def _():
                width = fst.shape[2]
                for i in range(width // LANES):
                    lanes = slice(i * LANES, (i + 1) * LANES)
                    upscr[i] = fst[t, :, lanes].astype(F32).reshape(cside, 2 * fside, LANES)
                lowered = None
                for a in range(2):
                    for c in range(2):
                        for i in range(width // LANES):
                            part = upscr[i, :, pl.ds(a * fside + c, cside, stride=2), :]
                            part = part.reshape(cside * cside, LANES).astype(BF16)
                            start = (2 * a + c) * width + i * LANES
                            term = dot(part, wd[start : start + LANES, :])
                            lowered = term if lowered is None else lowered + term
                dbuf[t] = lowered.astype(BF16)
                send_down(t).start()

            @pl.when(jnp.logical_and(jnp.logical_not(turn), seg < nseg - 1))
            def _():
                send_fo(t).start()

        save_f(t).start()

        @pl.when(lower)
        def _():
            skf[hold_f + t] = dot(fst[t], mixf[...]).astype(BF16)

            @pl.when(hold_f + t < ticks)
            def _():
                send_skf(hold_f + t).start()

        return carry

    lax.fori_loop(0, ticks, tick, 0)

    def back_f(first, src):
        return pltpu.make_async_copy(src, fback_out.at[first], save_sem.at[2, first])

    def back_c(first, src):
        return pltpu.make_async_copy(src, cback_out.at[first], save_sem.at[3, first])

    lower_backs = [back_f(j, skf.at[ticks + j]) for j in range(hold_f)]
    lower_backs += [
        back_c(j, skc.at[ticks + j] if j < recv_c else zc) for j in range(hold_c)
    ]
    upper_backs = [
        back_f(j, skf.at[ticks + j] if j < recv_f else zf) for j in range(hold_f)
    ]
    upper_backs += [back_c(j, skc.at[ticks + j]) for j in range(hold_c)]

    @pl.when(lower)
    def _():
        if own_fine:
            own_pend(9, fine_pend, skf, own_fine).wait()
        for j in range(max(ticks - recv_c, 0), ticks):
            send_skc(j).wait_recv()
        for item in lower_backs:
            item.start()
        for j in range(ticks):
            send_skf(j).wait_send()
        for item in lower_backs:
            item.wait()

    @pl.when(upper)
    def _():
        if own_coarse:
            own_pend(10, coarse_pend, skc, own_coarse).wait()
        for j in range(max(ticks - recv_f, 0), ticks):
            send_skf(j).wait_recv()
        for item in upper_backs:
            item.start()
        for j in range(ticks):
            send_skc(j).wait_send()
        for item in upper_backs:
            item.wait()

    @pl.when(turn)
    def _():
        for t in range(ticks - 1):
            send_up(t).wait_send()

    @pl.when(jnp.logical_and(jnp.logical_not(turn), seg < nseg - 1))
    def _():
        for t in range(ticks - 1):
            send_fo(t).wait_send()

    for t in range(ticks - 1):
        send_co(t).wait_send()
    for t in range(ticks):
        whole(gotf.at[2 * t], statf_s.at[2 * t], gotf_r.at[2 * t]).wait_send()
        whole(gotf.at[2 * t + 1], statf_s.at[2 * t + 1], gotf_r.at[2 * t + 1]).wait_send()
        whole(gotc.at[t], statc_s.at[t], gotc_r.at[t]).wait_send()
        save_f(t).wait()
        save_c(t).wait()


def hand_over_kernel(*refs):
    count = (len(refs) - 2) // 3
    sources, results, held = refs[:count], refs[count : 2 * count], refs[2 * count : 3 * count]
    in_sem, out_sem = refs[3 * count :]
    taken, given = [], []
    for i in range(count):
        for j in range(held[i].shape[0]):
            taken.append(pltpu.make_async_copy(sources[i].at[j], held[i].at[j], in_sem.at[i, j]))
            given.append(pltpu.make_async_copy(held[i].at[j], results[i].at[j], out_sem.at[i, j]))
    for item in taken:
        item.start()
    for item, other in zip(taken, given):
        item.wait()
        other.start()
    for item in given:
        item.wait()


def hand_over(arrays):
    most = max(array.shape[0] for array in arrays)
    any_spec = pl.BlockSpec(memory_space=pl.ANY)
    return pl.pallas_call(
        hand_over_kernel,
        out_shape=tuple(jax.ShapeDtypeStruct(a.shape, a.dtype) for a in arrays),
        in_specs=[any_spec] * len(arrays),
        out_specs=(any_spec,) * len(arrays),
        scratch_shapes=[pltpu.VMEM(a.shape, a.dtype) for a in arrays]
        + [pltpu.SemaphoreType.DMA((len(arrays), most))] * 2,
    )(*arrays)


def on_device(
    fine_inflow, coarse_inflow, fine_entries, fine_pending, coarse_pending,
    fine_kernels, fine_mixing, fine_gains, fine_shifts,
    coarse_kernel, coarse_mixing, coarse_gains, coarse_shifts,
    descent_kernel, upsample_kernel,
):
    nseg = lax.axis_size("segment")
    ndp = lax.axis_size("dp")
    half = nseg // 2
    ticks = fine_entries.shape[0] + 1
    hold_f, hold_c = fine_pending.shape[1], coarse_pending.shape[1]
    recv_f, recv_c = 3 * half - hold_f, half - hold_c
    fside, fch = fine_inflow.shape[3], fine_inflow.shape[4]
    cside, cch = coarse_inflow.shape[3], coarse_inflow.shape[4]
    fcells, ccells = fside * fside, cside * cside
    dims = (nseg, ndp, ticks, fside, cside, hold_f, recv_f, hold_c, recv_c)
    frows, crows = 2 * fch // LANES, 2 * cch // LANES
    any_spec = pl.BlockSpec(memory_space=pl.ANY)
    vmem_spec = pl.BlockSpec(memory_space=pltpu.VMEM)
    dma = pltpu.SemaphoreType.DMA
    outs = pl.pallas_call(
        functools.partial(kernel, dims),
        out_shape=(
            jax.ShapeDtypeStruct((ticks, fcells, fch), BF16),
            jax.ShapeDtypeStruct((ticks, ccells, cch), BF16),
            jax.ShapeDtypeStruct((hold_f, fcells, fch), BF16),
            jax.ShapeDtypeStruct((hold_c, ccells, cch), BF16),
        ),
        in_specs=[any_spec] * 7 + [vmem_spec] * 2 + [any_spec] * 2 + [vmem_spec] * 2 + [any_spec] * 2,
        out_specs=(any_spec,) * 4,
        scratch_shapes=[
            pltpu.VMEM((2, 9 * fch, fch), BF16),
            pltpu.VMEM((fch, fch), BF16),
            pltpu.VMEM((9 * cch, cch), BF16),
            pltpu.VMEM((cch, cch), BF16),
            pltpu.VMEM((4 * fch, cch), BF16),
            pltpu.VMEM((cch, 4 * fch), BF16),
            pltpu.VMEM((ticks, fcells, fch), BF16),
            pltpu.VMEM((ticks, ccells, cch), BF16),
            pltpu.VMEM((ticks, ccells, cch), BF16),
            pltpu.VMEM((max(hold_f, recv_f) + ticks, fcells, fch), BF16),
            pltpu.VMEM((max(hold_c, recv_c) + ticks, ccells, cch), BF16),
            pltpu.VMEM((ticks, fcells, fch), BF16),
            pltpu.VMEM((ticks, ccells, cch), BF16),
            pltpu.VMEM((ticks, ccells, cch), BF16),
            pltpu.VMEM((fcells, fch), F32),
            pltpu.VMEM((fcells, fch), F32),
            pltpu.VMEM((ccells, cch), F32),
            pltpu.VMEM((fch // LANES, cside, 2 * fside, LANES), F32),
            pltpu.VMEM((fcells, 9 * fch), BF16),
            pltpu.VMEM((ccells, 9 * cch), BF16),
            pltpu.VMEM((fcells, fch), BF16),
            pltpu.VMEM((ccells, cch), BF16),
            pltpu.VMEM((2 * ticks, frows, LANES), F32),
            pltpu.VMEM((ticks, crows, LANES), F32),
            pltpu.VMEM((2 * ticks, ndp - 1, frows, LANES), F32),
            pltpu.VMEM((ticks, ndp - 1, crows, LANES), F32),
            pltpu.VMEM((cch, 2, 2, fch), BF16),
            pltpu.VMEM((fch // LANES, 256, LANES), F32),
            dma((12,)),
            dma((4, max(ticks, hold_f, hold_c))),
            dma((ticks,)), dma((ticks,)), dma((ticks,)), dma((ticks,)), dma((ticks,)),
            dma((ticks,)), dma((ticks,)), dma((ticks,)), dma((ticks,)), dma((ticks,)),
            dma((2 * ticks,)), dma((ticks,)), dma((2 * ticks,)), dma((ticks,)),
        ],
        compiler_params=pltpu.CompilerParams(
            collective_id=0, has_side_effects=True, vmem_limit_bytes=56 << 20
        ),
    )(
        fine_inflow.reshape(fcells, fch),
        coarse_inflow.reshape(ccells, cch),
        fine_entries.reshape(ticks - 1, fcells, fch),
        fine_pending.reshape(hold_f, fcells, fch),
        coarse_pending.reshape(hold_c, ccells, cch),
        fine_kernels.reshape(2, 9 * fch, fch),
        fine_mixing.reshape(fch, fch),
        fine_gains.reshape(2, fch),
        fine_shifts.reshape(2, fch),
        coarse_kernel.reshape(9 * cch, cch),
        coarse_mixing.reshape(cch, cch),
        coarse_gains.reshape(1, cch),
        coarse_shifts.reshape(1, cch),
        descent_kernel.reshape(4 * fch, cch),
        upsample_kernel,
    )
    fst, cst, fback, cback = hand_over(outs)
    return (
        fst.reshape(1, ticks, 1, fside, fside, fch),
        cst.reshape(1, ticks, 1, cside, cside, cch),
        fback.reshape(1, hold_f, 1, fside, fside, fch),
        cback.reshape(1, hold_c, 1, cside, cside, cch),
    )


def solution(mesh):
    placed = (
        P("segment", "dp", None, None, None),
        P("segment", "dp", None, None, None),
        P(None, "dp", None, None, None),
        P("segment", None, "dp", None, None, None),
        P("segment", None, "dp", None, None, None),
        P("segment", None, None, None, None, None),
        P("segment", None, None),
        P("segment", None, None),
        P("segment", None, None),
        P("segment", None, None, None, None),
        P("segment", None, None),
        P("segment", None),
        P("segment", None),
        P(),
        P(),
    )
    return jax.shard_map(
        on_device,
        mesh=mesh,
        in_specs=placed,
        out_specs=(
            P("segment", None, "dp", None, None, None),
            P("segment", None, "dp", None, None, None),
            P("segment", None, "dp", None, None, None),
            P("segment", None, "dp", None, None, None),
        ),
        check_vma=False,
    )
```

```python
import functools

import jax
import jax.numpy as jnp
from jax import lax
from jax.experimental import pallas as pl
from jax.experimental.pallas import tpu as pltpu
from jax.sharding import PartitionSpec as P

EPSILON = 1e-05
LANES = 128
MESH = pl.DeviceIdType.MESH
F32 = jnp.float32
BF16 = jnp.bfloat16


def dot(a, b):
    return jnp.dot(a, b, preferred_element_type=F32)


def side_shifts(x, side):
    cells = x.shape[0]
    column = lax.rem(lax.broadcasted_iota(jnp.int32, x.shape, 0), side)
    before = jnp.where(column == 0, 0.0, pltpu.roll(x, 1, 0))
    after = jnp.where(column == side - 1, 0.0, pltpu.roll(x, cells - 1, 0))
    return before, x, after


def spread_taps(x, cols, side):
    cells, width = x.shape
    edge = jnp.zeros((side, width), F32)
    for dc, part in enumerate(side_shifts(x, side)):
        above = jnp.concatenate([edge, part[: cells - side]], axis=0)
        below = jnp.concatenate([part[side:], edge], axis=0)
        for dr, moved in enumerate((above, part, below)):
            start = (3 * dr + dc) * width
            cols[:, start : start + width] = moved.astype(BF16)


def put_stats(h, out):
    width = h.shape[1]
    rows = width // LANES
    total = jnp.sum(h, axis=0, keepdims=True)
    square = jnp.sum(h * h, axis=0, keepdims=True)
    for row in range(rows):
        lanes = slice(row * LANES, (row + 1) * LANES)
        out[row : row + 1, :] = total[:, lanes]
        out[rows + row : rows + row + 1, :] = square[:, lanes]


def norm_terms(total, gain, shift, count):
    rows = total.shape[0] // 2
    sums = jnp.concatenate([total[row : row + 1] for row in range(rows)], axis=1)
    squares = jnp.concatenate([total[rows + row : rows + row + 1] for row in range(rows)], axis=1)
    center = sums * (1.0 / count)
    spread = jnp.maximum(squares * (1.0 / count) - center * center, 0.0)
    scale = lax.rsqrt(spread + EPSILON) * gain
    return scale, shift - center * scale


def kernel(
    dims,
    fine_in, coarse_in, entries, fine_pend, coarse_pend,
    wf_hbm, mixf_hbm, fgain, fshift, wc_hbm, mixc_hbm, cgain, cshift, wd_hbm, wu_hbm,
    fst_out, cst_out, fback_out, cback_out,
    wf, mixf, wc, mixc, wd, wu,
    fin, cin, upin, skf, skc, fst, cst, dbuf,
    xs, hf, hg, hc, upscr, colf, colc, zf, zc,
    statf, statc, gotf, gotc,
    wu4, wuf, load_sem, save_sem,
    fin_r, cin_r, up_r, skf_r, skc_r,
    fin_s, cin_s, up_s, skf_s, skc_s,
    gotf_r, gotc_r, statf_s, statc_s,
):
    nseg, ndp, ticks, fside, cside, hold_f, recv_f, hold_c, recv_c = dims
    half = nseg // 2
    seg = lax.axis_index("segment")
    me = lax.axis_index("dp")
    lower = seg < half
    upper = seg >= half
    turn = seg == half - 1
    after = lax.rem(seg + 1, nseg)
    mate = lax.rem(seg + half, nseg)

    def load(k, src, dst):
        return pltpu.make_async_copy(src, dst, load_sem.at[k])

    get_fine = load(0, fine_in, fin.at[0])
    get_wf0 = load(1, wf_hbm.at[0], wf.at[0])
    get_mixf = load(2, mixf_hbm, mixf)
    get_coarse = load(3, coarse_in, cin.at[0])
    get_mixc = load(4, mixc_hbm, mixc)
    get_wc = load(5, wc_hbm, wc)
    get_wf1 = load(6, wf_hbm.at[1], wf.at[1])
    get_wd = load(7, wd_hbm, wd)
    get_wu = load(11, wu_hbm, wu4)
    own_entries = load(8, entries, fin.at[pl.ds(1, ticks - 1)])
    own_fine = hold_f if hold_f > ticks else 0
    own_coarse = hold_c if hold_c > ticks else 0

    def own_pend(k, src, dst, count):
        return load(k, src.at[pl.ds(0, count)], dst.at[pl.ds(0, count)])

    barrier = pltpu.get_barrier_semaphore()
    offsets = sorted({1 % nseg, nseg - 1, half})

    def greet(k, carry):
        pl.semaphore_signal(
            barrier, inc=1, device_id=(seg, lax.rem(me + k, ndp)), device_id_type=MESH
        )
        return carry

    lax.fori_loop(1, ndp, greet, 0)
    for offset in offsets:
        pl.semaphore_signal(
            barrier, inc=1, device_id=(lax.rem(seg + offset, nseg), me), device_id_type=MESH
        )
    @pl.when(upper)
    def _():
        if recv_f:
            own_pend(9, fine_pend, skf, recv_f).start()

    for item in (get_fine, get_wf0, get_mixf, get_coarse, get_mixc, get_wc, get_wf1):
        item.start()

    @pl.when(lower)
    def _():
        if recv_c:
            own_pend(10, coarse_pend, skc, recv_c).start()
        if own_fine:
            own_pend(9, fine_pend, skf, own_fine).start()

    @pl.when(upper)
    def _():
        if own_coarse:
            own_pend(10, coarse_pend, skc, own_coarse).start()

    @pl.when(seg == 0)
    def _():
        own_entries.start()

    @pl.when(turn)
    def _():
        get_wd.start()

    @pl.when(seg == half)
    def _():
        get_wu.start()

    zf[...] = jnp.zeros_like(zf)
    zc[...] = jnp.zeros_like(zc)
    pl.semaphore_wait(barrier, ndp - 1 + len(offsets))

    def push(src, dst, ssem, rsem, to):
        return pltpu.make_async_remote_copy(
            src_ref=src, dst_ref=dst, send_sem=ssem, recv_sem=rsem,
            device_id=(to, me), device_id_type=MESH,
        )

    def send_skf(j):
        return push(skf.at[j], skf.at[recv_f + j], skf_s.at[j], skf_r.at[j], mate)

    def send_pend_f(j):
        return push(fine_pend.at[j], skf.at[recv_f + j], skf_s.at[j], skf_r.at[j], mate)

    def send_pend_c(j):
        return push(coarse_pend.at[j], skc.at[recv_c + j], skc_s.at[j], skc_r.at[j], mate)

    def send_skc(j):
        return push(skc.at[j], skc.at[recv_c + j], skc_s.at[j], skc_r.at[j], mate)

    def send_up(t):
        return push(cst.at[t], upin.at[t], up_s.at[t], up_r.at[t], after)

    def send_co(t):
        return push(cst.at[t], cin.at[t + 1], cin_s.at[t], cin_r.at[t], after)

    def send_down(t):
        return push(dbuf.at[t], cin.at[t + 1], cin_s.at[t], cin_r.at[t], after)

    def send_fo(t):
        return push(fst.at[t], fin.at[t + 1], fin_s.at[t], fin_r.at[t], after)

    def exchange(src, dst, ssem, rsem):
        def one(k, carry):
            pltpu.make_async_remote_copy(
                src_ref=src, dst_ref=dst.at[k - 1], send_sem=ssem, recv_sem=rsem,
                device_id=(seg, lax.rem(me + k, ndp)), device_id_type=MESH,
            ).start()
            return carry

        lax.fori_loop(1, ndp, one, 0)

    def whole(dst, ssem, rsem):
        return pltpu.make_async_remote_copy(
            src_ref=dst, dst_ref=dst, send_sem=ssem, recv_sem=rsem,
            device_id=(seg, lax.rem(me + 1, ndp)), device_id_type=MESH,
        )

    @pl.when(lower)
    def _():
        for j in range(min(hold_f, ticks)):
            send_pend_f(j).start()

    @pl.when(upper)
    def _():
        for j in range(min(hold_c, ticks)):
            send_pend_c(j).start()

    fcount = ndp * fside * fside
    ccount = ndp * cside * cside

    def save_f(t):
        return pltpu.make_async_copy(fst.at[t], fst_out.at[t], save_sem.at[0, t])

    def save_c(t):
        return pltpu.make_async_copy(cst.at[t], cst_out.at[t], save_sem.at[1, t])

    def first(t, *items):
        @pl.when(t == 0)
        def _():
            for item in items:
                item.wait()

    def front(t):
        first(t, get_fine, get_mixf)

        @pl.when(lower)
        def _():
            @pl.when(jnp.logical_and(seg > 0, t > 0))
            def _():
                send_fo(t - 1).wait_recv()

            xs[...] = fin[t].astype(F32)

        @pl.when(upper)
        def _():
            @pl.when(jnp.logical_and(seg == half, t > 0))
            def _():
                send_up(t - 1).wait_recv()
                spread = dot(upin[t - 1], wu[...])
                width = spread.shape[1] // 4
                for a in range(2):
                    for c in range(2):
                        start = (2 * a + c) * width
                        part = spread[:, start : start + width].reshape(cside, cside, width)
                        for i in range(width // LANES):
                            lanes = slice(i * LANES, (i + 1) * LANES)
                            upscr[i, :, pl.ds(a * fside + c, cside, stride=2), :] = part[:, :, lanes]
                for i in range(width // LANES):
                    lanes = slice(i * LANES, (i + 1) * LANES)
                    fin[t, :, lanes] = upscr[i].reshape(fside * fside, LANES).astype(BF16)

            @pl.when(jnp.logical_and(seg != half, t > 0))
            def _():
                send_fo(t - 1).wait_recv()

            if recv_f:
                first(t, own_pend(9, fine_pend, skf, recv_f))

            @pl.when(t >= recv_f)
            def _():
                send_skf(t - recv_f).wait_recv()

            xs[...] = (dot(fin[t], mixf[...]) + skf[t].astype(F32)).astype(BF16).astype(F32)

        spread_taps(xs[...], colf, fside)
        first(t, get_wf0)
        hf[...] = dot(colf[...], wf[0])
        put_stats(hf[...], statf.at[2 * t])
        exchange(statf.at[2 * t], gotf.at[2 * t], statf_s.at[2 * t], gotf_r.at[2 * t])

    def later(which, t):
        @pl.when(jnp.logical_and(which, t < ticks - 1))
        def _():
            front(t + 1)

    def own_pieces(t):
        @pl.when(t == 0)
        def _():
            get_wf1.wait()

            @pl.when(turn)
            def _():
                get_wd.wait()

            @pl.when(seg == 0)
            def _():
                own_entries.wait()

            @pl.when(seg == half)
            def _():
                get_wu.wait()
                width = wu4.shape[3]
                depth = wuf.shape[1] // 4

                def rows_of(n, carry):
                    rows = pl.multiple_of(n * depth, depth)
                    piece = wu4[pl.ds(rows, depth)].astype(F32).reshape(4 * depth, width)
                    for i in range(width // LANES):
                        wuf[i] = piece[:, i * LANES : (i + 1) * LANES]
                    for q in range(4):
                        for i in range(width // LANES):
                            start = q * width + i * LANES
                            part = wuf[i, pl.ds(q, depth, stride=4), :]
                            wu[pl.ds(rows, depth), start : start + LANES] = part.astype(BF16)
                    return carry

                lax.fori_loop(0, wu4.shape[0] // depth, rows_of, 0)

    front(jnp.int32(0))
    own_pieces(jnp.int32(0))

    def tick(t, carry):
        first(t, get_coarse, get_mixc)

        @pl.when(t > 0)
        def _():
            send_co(t - 1).wait_recv()

        @pl.when(lower)
        def _():
            if recv_c:
                first(t, own_pend(10, coarse_pend, skc, recv_c))

            @pl.when(t >= recv_c)
            def _():
                send_skc(t - recv_c).wait_recv()

            hc[...] = (dot(cin[t], mixc[...]) + skc[t].astype(F32)).astype(BF16).astype(F32)

        @pl.when(upper)
        def _():
            hc[...] = cin[t].astype(F32)

        spread_taps(hc[...], colc, cside)
        first(t, get_wc)
        hc[...] = dot(colc[...], wc[...])
        put_stats(hc[...], statc.at[t])
        exchange(statc.at[t], gotc.at[t], statc_s.at[t], gotc_r.at[t])

        whole(gotf.at[2 * t], statf_s.at[2 * t], gotf_r.at[2 * t]).wait_recv()
        total = statf[2 * t] + jnp.sum(gotf[2 * t], axis=0)
        scale, offset = norm_terms(total, fgain[0:1, :], fshift[0:1, :], fcount)
        xs[...] = jnp.maximum(hf[...] * scale + offset, 0.0).astype(BF16).astype(F32)
        spread_taps(xs[...], colf, fside)
        hg[...] = dot(colf[...], wf[1])
        put_stats(hg[...], statf.at[2 * t + 1])
        exchange(
            statf.at[2 * t + 1], gotf.at[2 * t + 1], statf_s.at[2 * t + 1], gotf_r.at[2 * t + 1]
        )

        whole(gotc.at[t], statc_s.at[t], gotc_r.at[t]).wait_recv()
        total = statc[t] + jnp.sum(gotc[t], axis=0)
        scale, offset = norm_terms(total, cgain[...], cshift[...], ccount)
        cst[t] = jnp.maximum(hc[...] * scale + offset, 0.0).astype(BF16)

        @pl.when(t < ticks - 1)
        def _():
            @pl.when(turn)
            def _():
                send_up(t).start()

            @pl.when(jnp.logical_not(turn))
            def _():
                send_co(t).start()

        save_c(t).start()

        @pl.when(upper)
        def _():
            skc[hold_c + t] = dot(cst[t], mixc[...]).astype(BF16)

            @pl.when(hold_c + t < ticks)
            def _():
                send_skc(hold_c + t).start()

        later(seg == 0, t)

        whole(gotf.at[2 * t + 1], statf_s.at[2 * t + 1], gotf_r.at[2 * t + 1]).wait_recv()
        total = statf[2 * t + 1] + jnp.sum(gotf[2 * t + 1], axis=0)
        scale, offset = norm_terms(total, fgain[1:2, :], fshift[1:2, :], fcount)
        fst[t] = jnp.maximum(hg[...] * scale + offset, 0.0).astype(BF16)

        @pl.when(t < ticks - 1)
        def _():
            @pl.when(turn)
            def _():
                width = fst.shape[2]
                for i in range(width // LANES):
                    lanes = slice(i * LANES, (i + 1) * LANES)
                    upscr[i] = fst[t, :, lanes].astype(F32).reshape(cside, 2 * fside, LANES)
                lowered = None
                for a in range(2):
                    for c in range(2):
                        for i in range(width // LANES):
                            part = upscr[i, :, pl.ds(a * fside + c, cside, stride=2), :]
                            part = part.reshape(cside * cside, LANES).astype(BF16)
                            start = (2 * a + c) * width + i * LANES
                            term = dot(part, wd[start : start + LANES, :])
                            lowered = term if lowered is None else lowered + term
                dbuf[t] = lowered.astype(BF16)
                send_down(t).start()

            @pl.when(jnp.logical_and(jnp.logical_not(turn), seg < nseg - 1))
            def _():
                send_fo(t).start()

        save_f(t).start()

        @pl.when(lower)
        def _():
            skf[hold_f + t] = dot(fst[t], mixf[...]).astype(BF16)

            @pl.when(hold_f + t < ticks)
            def _():
                send_skf(hold_f + t).start()

        later(seg > 0, t)
        return carry

    lax.fori_loop(0, ticks, tick, 0)

    def back_f(first, src):
        return pltpu.make_async_copy(src, fback_out.at[first], save_sem.at[2, first])

    def back_c(first, src):
        return pltpu.make_async_copy(src, cback_out.at[first], save_sem.at[3, first])

    lower_backs = [back_f(j, skf.at[ticks + j]) for j in range(hold_f)]
    lower_backs += [
        back_c(j, skc.at[ticks + j] if j < recv_c else zc) for j in range(hold_c)
    ]
    upper_backs = [
        back_f(j, skf.at[ticks + j] if j < recv_f else zf) for j in range(hold_f)
    ]
    upper_backs += [back_c(j, skc.at[ticks + j]) for j in range(hold_c)]

    @pl.when(lower)
    def _():
        if own_fine:
            own_pend(9, fine_pend, skf, own_fine).wait()
        for j in range(max(ticks - recv_c, 0), ticks):
            send_skc(j).wait_recv()
        for item in lower_backs:
            item.start()
        for j in range(ticks):
            send_skf(j).wait_send()
        for item in lower_backs:
            item.wait()

    @pl.when(upper)
    def _():
        if own_coarse:
            own_pend(10, coarse_pend, skc, own_coarse).wait()
        for j in range(max(ticks - recv_f, 0), ticks):
            send_skf(j).wait_recv()
        for item in upper_backs:
            item.start()
        for j in range(ticks):
            send_skc(j).wait_send()
        for item in upper_backs:
            item.wait()

    @pl.when(turn)
    def _():
        for t in range(ticks - 1):
            send_up(t).wait_send()

    @pl.when(jnp.logical_and(jnp.logical_not(turn), seg < nseg - 1))
    def _():
        for t in range(ticks - 1):
            send_fo(t).wait_send()

    for t in range(ticks - 1):
        send_co(t).wait_send()
    for t in range(ticks):
        whole(gotf.at[2 * t], statf_s.at[2 * t], gotf_r.at[2 * t]).wait_send()
        whole(gotf.at[2 * t + 1], statf_s.at[2 * t + 1], gotf_r.at[2 * t + 1]).wait_send()
        whole(gotc.at[t], statc_s.at[t], gotc_r.at[t]).wait_send()
        save_f(t).wait()
        save_c(t).wait()


def hand_over_kernel(*refs):
    count = (len(refs) - 2) // 3
    sources, results, held = refs[:count], refs[count : 2 * count], refs[2 * count : 3 * count]
    in_sem, out_sem = refs[3 * count :]
    taken, given = [], []
    for i in range(count):
        for j in range(held[i].shape[0]):
            taken.append(pltpu.make_async_copy(sources[i].at[j], held[i].at[j], in_sem.at[i, j]))
            given.append(pltpu.make_async_copy(held[i].at[j], results[i].at[j], out_sem.at[i, j]))
    for item in taken:
        item.start()
    for item, other in zip(taken, given):
        item.wait()
        other.start()
    for item in given:
        item.wait()


def hand_over(arrays):
    most = max(array.shape[0] for array in arrays)
    any_spec = pl.BlockSpec(memory_space=pl.ANY)
    return pl.pallas_call(
        hand_over_kernel,
        out_shape=tuple(jax.ShapeDtypeStruct(a.shape, a.dtype) for a in arrays),
        in_specs=[any_spec] * len(arrays),
        out_specs=(any_spec,) * len(arrays),
        scratch_shapes=[pltpu.VMEM(a.shape, a.dtype) for a in arrays]
        + [pltpu.SemaphoreType.DMA((len(arrays), most))] * 2,
    )(*arrays)


def on_device(
    fine_inflow, coarse_inflow, fine_entries, fine_pending, coarse_pending,
    fine_kernels, fine_mixing, fine_gains, fine_shifts,
    coarse_kernel, coarse_mixing, coarse_gains, coarse_shifts,
    descent_kernel, upsample_kernel,
):
    nseg = lax.axis_size("segment")
    ndp = lax.axis_size("dp")
    half = nseg // 2
    ticks = fine_entries.shape[0] + 1
    hold_f, hold_c = fine_pending.shape[1], coarse_pending.shape[1]
    recv_f, recv_c = 3 * half - hold_f, half - hold_c
    fside, fch = fine_inflow.shape[3], fine_inflow.shape[4]
    cside, cch = coarse_inflow.shape[3], coarse_inflow.shape[4]
    fcells, ccells = fside * fside, cside * cside
    dims = (nseg, ndp, ticks, fside, cside, hold_f, recv_f, hold_c, recv_c)
    frows, crows = 2 * fch // LANES, 2 * cch // LANES
    any_spec = pl.BlockSpec(memory_space=pl.ANY)
    vmem_spec = pl.BlockSpec(memory_space=pltpu.VMEM)
    dma = pltpu.SemaphoreType.DMA
    outs = pl.pallas_call(
        functools.partial(kernel, dims),
        out_shape=(
            jax.ShapeDtypeStruct((ticks, fcells, fch), BF16),
            jax.ShapeDtypeStruct((ticks, ccells, cch), BF16),
            jax.ShapeDtypeStruct((hold_f, fcells, fch), BF16),
            jax.ShapeDtypeStruct((hold_c, ccells, cch), BF16),
        ),
        in_specs=[any_spec] * 7 + [vmem_spec] * 2 + [any_spec] * 2 + [vmem_spec] * 2 + [any_spec] * 2,
        out_specs=(any_spec,) * 4,
        scratch_shapes=[
            pltpu.VMEM((2, 9 * fch, fch), BF16),
            pltpu.VMEM((fch, fch), BF16),
            pltpu.VMEM((9 * cch, cch), BF16),
            pltpu.VMEM((cch, cch), BF16),
            pltpu.VMEM((4 * fch, cch), BF16),
            pltpu.VMEM((cch, 4 * fch), BF16),
            pltpu.VMEM((ticks, fcells, fch), BF16),
            pltpu.VMEM((ticks, ccells, cch), BF16),
            pltpu.VMEM((ticks, ccells, cch), BF16),
            pltpu.VMEM((max(hold_f, recv_f) + ticks, fcells, fch), BF16),
            pltpu.VMEM((max(hold_c, recv_c) + ticks, ccells, cch), BF16),
            pltpu.VMEM((ticks, fcells, fch), BF16),
            pltpu.VMEM((ticks, ccells, cch), BF16),
            pltpu.VMEM((ticks, ccells, cch), BF16),
            pltpu.VMEM((fcells, fch), F32),
            pltpu.VMEM((fcells, fch), F32),
            pltpu.VMEM((fcells, fch), F32),
            pltpu.VMEM((ccells, cch), F32),
            pltpu.VMEM((fch // LANES, cside, 2 * fside, LANES), F32),
            pltpu.VMEM((fcells, 9 * fch), BF16),
            pltpu.VMEM((ccells, 9 * cch), BF16),
            pltpu.VMEM((fcells, fch), BF16),
            pltpu.VMEM((ccells, cch), BF16),
            pltpu.VMEM((2 * ticks, frows, LANES), F32),
            pltpu.VMEM((ticks, crows, LANES), F32),
            pltpu.VMEM((2 * ticks, ndp - 1, frows, LANES), F32),
            pltpu.VMEM((ticks, ndp - 1, crows, LANES), F32),
            pltpu.VMEM((cch, 2, 2, fch), BF16),
            pltpu.VMEM((fch // LANES, 256, LANES), F32),
            dma((12,)),
            dma((4, max(ticks, hold_f, hold_c))),
            dma((ticks,)), dma((ticks,)), dma((ticks,)), dma((ticks,)), dma((ticks,)),
            dma((ticks,)), dma((ticks,)), dma((ticks,)), dma((ticks,)), dma((ticks,)),
            dma((2 * ticks,)), dma((ticks,)), dma((2 * ticks,)), dma((ticks,)),
        ],
        compiler_params=pltpu.CompilerParams(
            collective_id=0, has_side_effects=True, vmem_limit_bytes=56 << 20
        ),
    )(
        fine_inflow.reshape(fcells, fch),
        coarse_inflow.reshape(ccells, cch),
        fine_entries.reshape(ticks - 1, fcells, fch),
        fine_pending.reshape(hold_f, fcells, fch),
        coarse_pending.reshape(hold_c, ccells, cch),
        fine_kernels.reshape(2, 9 * fch, fch),
        fine_mixing.reshape(fch, fch),
        fine_gains.reshape(2, fch),
        fine_shifts.reshape(2, fch),
        coarse_kernel.reshape(9 * cch, cch),
        coarse_mixing.reshape(cch, cch),
        coarse_gains.reshape(1, cch),
        coarse_shifts.reshape(1, cch),
        descent_kernel.reshape(4 * fch, cch),
        upsample_kernel,
    )
    fst, cst, fback, cback = hand_over(outs)
    return (
        fst.reshape(1, ticks, 1, fside, fside, fch),
        cst.reshape(1, ticks, 1, cside, cside, cch),
        fback.reshape(1, hold_f, 1, fside, fside, fch),
        cback.reshape(1, hold_c, 1, cside, cside, cch),
    )


def solution(mesh):
    placed = (
        P("segment", "dp", None, None, None),
        P("segment", "dp", None, None, None),
        P(None, "dp", None, None, None),
        P("segment", None, "dp", None, None, None),
        P("segment", None, "dp", None, None, None),
        P("segment", None, None, None, None, None),
        P("segment", None, None),
        P("segment", None, None),
        P("segment", None, None),
        P("segment", None, None, None, None),
        P("segment", None, None),
        P("segment", None),
        P("segment", None),
        P(),
        P(),
    )
    return jax.shard_map(
        on_device,
        mesh=mesh,
        in_specs=placed,
        out_specs=(
            P("segment", None, "dp", None, None, None),
            P("segment", None, "dp", None, None, None),
            P("segment", None, "dp", None, None, None),
            P("segment", None, "dp", None, None, None),
        ),
        check_vma=False,
    )
```
